128 devices in a mesh: dom: 32 (over y, x, core), near: 4 (over z).
Axes of the slice: x: 4, y: 4, z: 4, core: 2. Of those that a mesh axis runs over, the one named last changes fastest.
Arguments:
- start_block: float32 [131072, 128], P(('dom', 'near')), may hold values from -6 to 6
- near_tiles: float32 [6144, 128, 128], P(('dom', 'near')), may hold values from -0.09375 to 0.09375
- near_src: int32 [6144], P(('dom', 'near')), may hold values from 0 to 31, as said below
- near_mask: int32 [6144], P(('dom', 'near')), may hold values 0 or 1
- far_tiles: float32 [1024, 128, 128], P(('dom', 'near')), may hold values from -0.09375 to 0.09375
- far_src: int32 [1024], P(('dom', 'near')), may hold values from 0 to 31
- far_mask: int32 [1024], P(('dom', 'near')), may hold values 0 or 1
- bound_count: int32 [128], P(('dom', 'near')), may hold values from 1 to 128
Outputs:
- encodings: float32 [131072, 128], P(('dom', 'near'))
- rayleigh: float32 [128, 128], replicated
The draws below stay inside these ranges and needn't reach their ends.
Inputs may be any that keep to these rules, and one draw needn't show every extreme that they name: `near_src`: each partition holds 48 consecutive slots; the slot at position j among them (j from 0) lies in tile row j // 6; the first slot of each tile row reads the partition's own tile of that row; every source tile from another partition of the group is one of that partition's first 4 tiles.
All inputs are finite; a program needn't handle non-finite values. No bound on the sum of `near_mask` or of `far_mask` on one device may be relied on, other than what follows from the above.
Results may differ from the reference program's by a relative error of at most 0.0003.
Values sent between devices are 32-bit elements; how exact they have to be, the bound alone decides.
No kernel may reach another device: no remote copies, remote signals or barrier semaphores. Data moves between devices by JAX's collectives and lax.ppermute only.
A program may use at most 64 MiB of HBM per device.

```python
import jax
import jax.numpy as jnp
from jax import lax

K = 128
TB = 128
TILES_DEV = 8
NPER = 6
NBT = 4
ITERS = 2
DEG = 3
NODES = 131072
NEAR_SLOTS = 6144
FAR_SLOTS = 1024
N_DOM = 32
N_NEAR = 4
DEVICES = 128


def draw_near_src(key, part):
    total = DEVICES * NPER * TILES_DEV
    position = jnp.arange(total, dtype=jnp.int32)
    device = position // (NPER * TILES_DEV)
    slot = position % (NPER * TILES_DEV)
    tile_row = slot // NPER
    near_index = device % N_NEAR
    key_peer, key_own, key_border = jax.random.split(jax.random.fold_in(key, 17), 3)
    peer = jax.random.randint(key_peer, (total,), 0, N_NEAR, dtype=jnp.int32)
    own_tile = jax.random.randint(key_own, (total,), 0, TILES_DEV, dtype=jnp.int32)
    border_tile = jax.random.randint(key_border, (total,), 0, NBT, dtype=jnp.int32)
    chosen = jnp.where(peer == near_index, own_tile, border_tile)
    source = jnp.where(slot % NPER == 0, near_index * TILES_DEV + tile_row, peer * TILES_DEV + chosen)
    return source.astype(jnp.int32)


def touch_ends(values, key, smallest, top_value):
    dims = values.shape
    spot = [jax.random.randint(jax.random.fold_in(key, axis), (), 0, dims[axis]) for axis in range(len(dims))]
    values = values.at[tuple(spot)].set(smallest)
    longest = dims.index(max(dims))
    spot[longest] = (spot[longest] + 1) % dims[longest]
    return values.at[tuple(spot)].set(top_value)


def block_levels(own_key, extent, cuts, least, top_value):
    def one(dim, shards_of):
        steps = jax.random.uniform(jax.random.fold_in(jax.random.fold_in(own_key, 6), dim), (shards_of,), jnp.float32, least / len(cuts), top_value / len(cuts))
        return jnp.repeat(jnp.exp(steps), extent[dim] // shards_of).reshape((-1,) + (1,) * (len(extent) - dim - 1))

    gain = one(*cuts[0])
    for cut in cuts[1:]:
        gain = gain * one(*cut)
    return gain


def bell_draw(key, dims, spread, most, pieces=(), kind=jnp.bfloat16):
    array = jax.random.normal(key, dims, jnp.float32) * spread
    if len(pieces) > 0:
        array = block_levels(key, dims, pieces, -0.22, 0.18) * array
    return jnp.clip(array, min=-most, max=most).astype(kind)


def setup_inputs(seed: int = 0) -> dict:
    splits = jax.random.split(jax.random.key(seed), 9)
    return {
        "start_block": bell_draw(splits[0], (NODES, K), 1.0, 6.0, ((0, 128),), jnp.float32),
        "near_tiles": bell_draw(splits[1], (NEAR_SLOTS, TB, TB), (4 * (NPER + 1) * TB) ** -0.5, 0.09375, ((0, 128),), jnp.float32),
        "near_src": draw_near_src(jax.random.fold_in(splits[8], 71), 0),
        "near_mask": touch_ends((jax.random.randint(splits[3], (NEAR_SLOTS,), 0, 4) < 3).astype(jnp.int32), jax.random.fold_in(splits[3], 1), 0, 1),
        "far_tiles": bell_draw(splits[4], (FAR_SLOTS, TB, TB), (4 * (NPER + 1) * TB) ** -0.5, 0.09375, ((0, 128),), jnp.float32),
        "far_src": touch_ends(jax.random.randint(splits[5], (FAR_SLOTS,), 0, N_DOM), jax.random.fold_in(splits[5], 1), 0, N_DOM - 1).astype(jnp.int32),
        "far_mask": touch_ends((jax.random.randint(splits[6], (FAR_SLOTS,), 0, 4) < 3).astype(jnp.int32), jax.random.fold_in(splits[6], 1), 0, 1),
        "bound_count": touch_ends(jax.random.randint(splits[7], (DEVICES,), 1, TB + 1), jax.random.fold_in(splits[7], 1), 1, TB).astype(jnp.int32),
    }


LOWER_EDGE = 0.6
UPPER_EDGE = 2.0

def apply_all(block, near_tiles, near_src, near_mask, far_tiles, far_src, far_mask, bound_count):
    tile_rows = near_tiles.shape[1]
    width = block.shape[1]
    devices = bound_count.shape[0]
    tiles_dev = block.shape[0] // (devices * tile_rows)
    group_view = block.reshape(N_DOM, N_NEAR * tiles_dev, tile_rows, width)
    limit = (jnp.arange(tile_rows)[None, :] < bound_count[:, None]).astype(jnp.float32)
    edges = block.reshape(devices, tiles_dev, tile_rows, width)[:, 0] * limit[:, :, None]
    edges = edges.reshape(N_DOM, N_NEAR, tile_rows, width)
    own_view = block.reshape(devices, tiles_dev * tile_rows, width)

    def one_part(items):
        tiles, sources, masks, far_t, far_s, far_m, device = items
        dom_index = device // N_NEAR
        near_index = device % N_NEAR
        picked = group_view[dom_index][sources]
        products = jnp.einsum('sij,sjk->sik', tiles, picked, precision=lax.Precision.HIGHEST)
        products = products * masks.astype(jnp.float32)[:, None, None]
        near_sum = products.reshape(tiles_dev, NPER, tile_rows, width).sum(axis=1)
        far_pick = edges[far_s, near_index]
        far_sum = jnp.einsum('sij,sjk->sik', far_t, far_pick, precision=lax.Precision.HIGHEST)
        far_sum = far_sum * far_m.astype(jnp.float32)[:, None, None]
        return own_view[device] - (near_sum + far_sum).reshape(tiles_dev * tile_rows, width)
    items = (near_tiles.reshape(devices, NPER * tiles_dev, tile_rows, tile_rows), near_src.reshape(devices, -1), near_mask.reshape(devices, -1), far_tiles.reshape(devices, tiles_dev, tile_rows, tile_rows), far_src.reshape(devices, -1), far_mask.reshape(devices, -1), jnp.arange(devices, dtype=jnp.int32))
    return lax.map(one_part, items).reshape(block.shape)

def reference(start_block, near_tiles, near_src, near_mask, far_tiles, far_src, far_mask, bound_count):

    def operator(block):
        return apply_all(block, near_tiles, near_src, near_mask, far_tiles, far_src, far_mask, bound_count)
    center = (UPPER_EDGE + LOWER_EDGE) / 2.0
    half = (UPPER_EDGE - LOWER_EDGE) / 2.0
    nodes_all = start_block.shape[0]
    width = start_block.shape[1]
    current = start_block
    for iteration in range(ITERS):
        previous = current
        present = (operator(current) - center * current) / half
        for degree in range(DEG - 1):
            following = 2.0 * (operator(present) - center * present) / half - previous
            previous, present = (present, following)
        filtered = present
        gram = jnp.dot(filtered.T.astype(jnp.float32), filtered.astype(jnp.float32), precision=lax.Precision.HIGHEST, preferred_element_type=jnp.float32) / nodes_all
        lower = jnp.linalg.cholesky(gram)
        lower_inv = jax.scipy.linalg.solve_triangular(lower, jnp.eye(width, dtype=jnp.float32), lower=True)
        current = jnp.dot(filtered.astype(jnp.float32), lower_inv.T.astype(jnp.float32), precision=lax.Precision.HIGHEST, preferred_element_type=jnp.float32)
    image = operator(current)
    rayleigh = jnp.dot(current.T.astype(jnp.float32), image.astype(jnp.float32), precision=lax.Precision.HIGHEST, preferred_element_type=jnp.float32) / nodes_all
    return (current, rayleigh)
```

```python
from functools import partial

import jax
import jax.numpy as jnp
from jax import lax
from jax.experimental import pallas as pl
from jax.experimental.pallas import tpu as pltpu
from jax.sharding import PartitionSpec as P


TB = 128
NPER = 6
ROWS = 8
HEAD = 4
CENTER = 1.3
HALF = 0.7
NODES = 131072
AXES = ("dom", "near")
NEAR_BUFFERS = 8 + 3 * HEAD
CHIPS = 16


def pairs(dy=0, dx=0, dc=0, dz=0):
    out = []
    for y in range(4):
        for x in range(4):
            for c in range(2):
                for z in range(4):
                    there = (((y + dy) % 4) * 4 + (x + dx) % 4) * 2 + (c + dc) % 2
                    out.append((((y * 4 + x) * 2 + c) * 4 + z, there * 4 + (z + dz) % 4))
    return out


def shift(value, **step):
    return lax.ppermute(value, AXES, pairs(**step))


def same_core():
    return [[chip * 2 + c for chip in range(CHIPS)] for c in range(2)]


def split(x):
    hi = x.astype(jnp.bfloat16)
    lo = (x - hi.astype(jnp.float32)).astype(jnp.bfloat16)
    return hi, lo


def wide(x):
    return jnp.concatenate(split(x), axis=1)


def tall(x):
    return jnp.concatenate(split(x), axis=0)


def fold(acc):
    return (acc[:TB, :TB] + acc[TB:, TB:]) + (acc[:TB, TB:] + acc[TB:, :TB])


def dot(a, b, dims):
    return lax.dot_general(a, b, (dims, ((), ())), preferred_element_type=jnp.float32)


def prep_kernel(near_mask, far_mask, near_ref, far_ref, t_ref, tf_ref):
    r = pl.program_id(0)
    for s in range(NPER):
        tile = near_ref[s] * near_mask[r * NPER + s].astype(jnp.float32)
        hi, lo = split(tile)
        cols = pl.ds((s % 2) * TB, TB)
        t_ref[0, s // 2, pl.ds(0, TB), cols] = hi
        t_ref[0, s // 2, pl.ds(TB, TB), cols] = lo
    tile = far_ref[0] * far_mask[r].astype(jnp.float32)
    tf_ref[0] = tall(tile)


def prepare(near_tiles, near_mask, far_tiles, far_mask):
    return pl.pallas_call(
        prep_kernel,
        grid_spec=pltpu.PrefetchScalarGridSpec(
            num_scalar_prefetch=2,
            grid=(ROWS,),
            in_specs=[
                pl.BlockSpec((NPER, TB, TB), lambda r, *_: (r, 0, 0)),
                pl.BlockSpec((1, TB, TB), lambda r, *_: (r, 0, 0)),
            ],
            out_specs=[
                pl.BlockSpec((1, NPER // 2, 2 * TB, 2 * TB), lambda r, *_: (r, 0, 0, 0)),
                pl.BlockSpec((1, 2 * TB, TB), lambda r, *_: (r, 0, 0)),
            ],
        ),
        out_shape=[
            jax.ShapeDtypeStruct((ROWS, NPER // 2, 2 * TB, 2 * TB), jnp.bfloat16),
            jax.ShapeDtypeStruct((ROWS, 2 * TB, TB), jnp.bfloat16),
        ],
        name="prepare",
    )(near_mask, far_mask, near_tiles, far_tiles)


def apply_kernel(kind, coefs, *refs):
    index, bound, t_ref, tf_ref, head, tail = refs[:6]
    rest = list(refs[6:])
    own, times, back = coefs
    prev = (rest.pop(0), rest.pop(0)) if back else None
    halo = [rest.pop(0) for _ in range(3)]
    far = [rest.pop(0) for _ in range(2)]
    inverse = rest.pop(0) if kind == "norm" else None
    outs = rest
    v_ref = outs.pop()
    o_ref = outs.pop() if kind != "step" else None
    for t in range(ROWS):
        part = head if t < HEAD else tail
        v_ref[t] = wide(part[pl.ds((t % HEAD) * TB, TB), :])
    for b in range(3):
        for t in range(HEAD):
            v_ref[8 + b * HEAD + t] = wide(halo[b][pl.ds(t * TB, TB), :])
    for b in range(2):
        for t in range(CHIPS):
            v_ref[NEAR_BUFFERS + b * CHIPS + t] = wide(far[b][t])
    if inverse is not None:
        inv = wide_rows(inverse[...])
    for r in range(ROWS):
        acc = dot(tf_ref[r], v_ref[index[NPER * ROWS + r]], ((1,), (0,)))
        for p in range(NPER // 2):
            first = NPER * r + 2 * p
            rhs = jnp.concatenate([v_ref[index[first]], v_ref[index[first + 1]]], axis=0)
            acc = acc + dot(t_ref[r, p], rhs, ((1,), (0,)))
        part = head if r < HEAD else tail
        where = pl.ds((r % HEAD) * TB, TB)
        row = own * part[where, :] + times * fold(acc)
        if prev is not None:
            row = row - (prev[0] if r < HEAD else prev[1])[where, :]
        if inverse is not None:
            row = fold(dot(tall(row), inv, ((1,), (1,))))
        if kind != "step":
            o_ref[pl.ds(r * TB, TB), :] = wide(row)
        if kind != "last":
            (outs[0] if r < HEAD else outs[1])[where, :] = row
            if r == 0:
                rows = lax.broadcasted_iota(jnp.int32, (TB, TB), 0)
                edge = jnp.where(rows < bound[0], row, 0.0)
                for t in range(CHIPS):
                    outs[2][t] = edge
    if kind in ("gram", "norm"):
        outs[3][...] = fold(dot(o_ref[...], o_ref[...], ((0,), (0,))))
    if kind == "last":
        block = jnp.concatenate([v_ref[t] for t in range(ROWS)], axis=0)
        outs[0][...] = fold(dot(block, o_ref[...], ((0,), (0,))))


def wide_rows(x):
    return tall(x)


def apply(kind, coefs, index, bound, tiles, state, prev, halo, far, inverse=None):
    head = jax.ShapeDtypeStruct((HEAD * TB, TB), jnp.float32)
    small = jax.ShapeDtypeStruct((TB, TB), jnp.float32)
    edge = jax.ShapeDtypeStruct((CHIPS, TB, TB), jnp.float32)
    outs = {
        "step": [head, head, edge],
        "gram": [head, head, edge, small],
        "norm": [head, head, edge, small],
        "last": [small],
    }[kind]
    args = [index, bound, *tiles, *state]
    if prev is not None:
        args += prev
    args += [*halo, *far]
    if inverse is not None:
        args.append(inverse)
    vmem = pl.BlockSpec(memory_space=pltpu.MemorySpace.VMEM)
    smem = pl.BlockSpec(memory_space=pltpu.MemorySpace.SMEM)
    scratch = [] if kind == "step" else [pltpu.VMEM((ROWS * TB, 2 * TB), jnp.bfloat16)]
    scratch.append(pltpu.VMEM((NEAR_BUFFERS + 2 * CHIPS, TB, 2 * TB), jnp.bfloat16))
    return pl.pallas_call(
        partial(apply_kernel, kind, (*coefs, prev is not None)),
        in_specs=[smem, smem] + [vmem] * (len(args) - 2),
        out_specs=[vmem] * len(outs),
        out_shape=outs,
        scratch_shapes=scratch,
        name="apply_" + kind,
    )(*args)


def start_kernel(bound, block, head, tail, edge):
    head[...] = block[pl.ds(0, HEAD * TB), :]
    tail[...] = block[pl.ds(HEAD * TB, HEAD * TB), :]
    rows = lax.broadcasted_iota(jnp.int32, (TB, TB), 0)
    tile = jnp.where(rows < bound[0], block[pl.ds(0, TB), :], 0.0)
    for t in range(CHIPS):
        edge[t] = tile


def start(bound, block):
    vmem = pl.BlockSpec(memory_space=pltpu.MemorySpace.VMEM)
    head = jax.ShapeDtypeStruct((HEAD * TB, TB), jnp.float32)
    return pl.pallas_call(
        start_kernel,
        in_specs=[pl.BlockSpec(memory_space=pltpu.MemorySpace.SMEM), vmem],
        out_specs=[vmem] * 3,
        out_shape=[head, head, jax.ShapeDtypeStruct((CHIPS, TB, TB), jnp.float32)],
        name="begin",
    )(bound, block)


def final_kernel(head, tail, inverse, out):
    inv = wide_rows(inverse[...])
    for r in range(ROWS):
        part = head if r < HEAD else tail
        row = part[pl.ds((r % HEAD) * TB, TB), :]
        out[pl.ds(r * TB, TB), :] = fold(dot(tall(row), inv, ((1,), (1,))))


def final(state, inverse):
    vmem = pl.BlockSpec(memory_space=pltpu.MemorySpace.VMEM)
    return pl.pallas_call(
        final_kernel,
        in_specs=[vmem] * 3,
        out_specs=vmem,
        out_shape=jax.ShapeDtypeStruct((ROWS * TB, TB), jnp.float32),
        name="final",
    )(*state, inverse)


def exchange(head, edge):
    halo = [shift(head, dz=1), shift(head, dz=3), shift(head, dz=2)]
    mine = lax.all_to_all(edge, "dom", 0, 0, axis_index_groups=same_core())
    return halo, [mine, shift(mine, dc=1)]


def all_sum(value):
    value = value + shift(value, dc=1)
    for axis in ("dz", "dx", "dy"):
        one, three, two = (shift(value, **{axis: step}) for step in (1, 3, 2))
        value = (value + two) + (one + three)
    return value


def inverse_factor(gram):
    lower = jnp.linalg.cholesky(gram)
    eye = jnp.eye(gram.shape[0], dtype=jnp.float32)
    return jax.scipy.linalg.solve_triangular(lower, eye, lower=True)


def source_index(near_src, far_src):
    z = lax.axis_index("near")
    core = lax.axis_index("dom") % 2
    tile = near_src % ROWS
    away = (near_src // ROWS - z) % 4
    base = jnp.where(away == 3, 8, jnp.where(away == 1, 8 + HEAD, 8 + 2 * HEAD))
    near = jnp.where(away == 0, tile, base + jnp.minimum(tile, HEAD - 1))
    far = NEAR_BUFFERS + jnp.where(far_src % 2 == core, 0, CHIPS) + far_src // 2
    return jnp.concatenate([near, far]).astype(jnp.int32)


def local(start_block, near_tiles, near_src, near_mask, far_tiles, far_src, far_mask, bound_count):
    tiles = prepare(near_tiles, near_mask, far_tiles, far_mask)
    index = source_index(near_src, far_src)
    first = ((1.0 - CENTER) / HALF, -1.0 / HALF)
    later = (2.0 * first[0], 2.0 * first[1])

    def operate(kind, coefs, state, edge, prev, inverse=None):
        halo, far = exchange(state[0], edge)
        return apply(kind, coefs, index, bound_count, tiles, state, prev, halo, far, inverse)

    *state, edge = start(bound_count, start_block)
    inverse = None
    for iteration in range(2):
        *one, edge = operate("step", first, state, edge, None)
        *two, edge = operate("step", later, one, edge, state)
        kind = "gram" if iteration == 0 else "norm"
        *state, edge, gram = operate(kind, later, two, edge, one, inverse)
        inverse = inverse_factor(all_sum(gram) / NODES)
    (projection,) = operate("last", (1.0, -1.0), state, edge, None)
    encodings = final(state, inverse)
    projection = all_sum(projection) / NODES
    high = lax.Precision.HIGHEST
    left = jnp.dot(inverse, projection, precision=high)
    rayleigh = jnp.dot(left, inverse.T, precision=high)
    return encodings, rayleigh


def solution(mesh):
    rows = P(AXES)
    return jax.shard_map(
        local,
        mesh=mesh,
        in_specs=(rows,) * 8,
        out_specs=(rows, P()),
        check_vma=False,
    )
```

```python
from functools import partial

import jax
import jax.numpy as jnp
from jax import lax
from jax.experimental import pallas as pl
from jax.experimental.pallas import tpu as pltpu
from jax.sharding import PartitionSpec as P


TB = 128
NPER = 6
ROWS = 8
HEAD = 4
PANEL = 16
STEP = 2
CENTER = 1.3
HALF = 0.7
NODES = 131072
AXES = ("dom", "near")
NEAR_BUFFERS = 8 + 3 * HEAD
PARAMS = pltpu.CompilerParams(vmem_limit_bytes=8 << 20)


def pairs(first, second):
    out = []
    for y in range(4):
        for x in range(4):
            for c in range(2):
                for z in range(4):
                    dy, dx, dc, dz = second if c else first
                    there = (((y + dy) % 4) * 4 + (x + dx) % 4) * 2 + (c + dc) % 2
                    out.append((((y * 4 + x) * 2 + c) * 4 + z, there * 4 + (z + dz) % 4))
    return out


def shift(value, dy=0, dx=0, dc=0, dz=0):
    step = (dy, dx, dc, dz)
    return lax.ppermute(value, AXES, pairs(step, step))


def cross(value, along, stage):
    steps = ((0, along, 0, 0), (along, 0, 0, 0))
    return lax.ppermute(value, AXES, pairs(steps[stage], steps[1 - stage]))


def split(x):
    hi = x.astype(jnp.bfloat16)
    lo = (x - hi.astype(jnp.float32)).astype(jnp.bfloat16)
    return hi, lo


def wide(x):
    return jnp.concatenate(split(x), axis=1)


def tall(x):
    return jnp.concatenate(split(x), axis=0)


def fold(acc):
    return (acc[:TB, :TB] + acc[TB:, TB:]) + (acc[:TB, TB:] + acc[TB:, :TB])


def dot(a, b, dims):
    return lax.dot_general(a, b, (dims, ((), ())), preferred_element_type=jnp.float32)


def prep_kernel(near_src, near_mask, far_src, far_mask, here, near, far, own_ref, t_ref, table, near_v, far_v, sems):
    dom, z = here[0], here[1]
    core = dom & 1
    copies = [
        pltpu.make_async_copy(near.at[pl.ds(r * NPER, NPER)], near_v.at[pl.ds(r * NPER, NPER)], sems.at[r])
        for r in range(ROWS)
    ]
    copies.append(pltpu.make_async_copy(far, far_v, sems.at[ROWS]))
    for copy in copies:
        copy.start()

    def lookup(r, _):
        for s in range(NPER):
            if s < NPER - 1:
                source = near_src[r * NPER + s + 1]
                away = ((source >> 3) - z) & 3
                straight = jnp.where(core == 0, 3, 1)
                buffer = jnp.where(away == 2, 2, jnp.where(away == straight, 0, 1))
                halo = ROWS + buffer * HEAD + (source & 3)
                table[r * NPER + s] = jnp.where(away == 0, source & 7, halo)
            else:
                chip = far_src[r] >> 1
                dy = (0x78 >> 2 * (((chip >> 2) - (dom >> 3)) & 3)) & 3
                dx = (0x78 >> 2 * ((chip - (dom >> 1)) & 3)) & 3
                theirs = far_src[r] & 1
                inner = jnp.where(theirs == 0, dx, dy)
                outer = jnp.where(theirs == 0, dy, dx)
                piece = jnp.where(outer == 0, 0, jnp.where(outer == 3, 4, 8))
                swapped = jnp.where(outer == 2, inner * 8 + 5, (piece + inner) * 8 + 4)
                table[r * NPER + s] = jnp.where(theirs == core, inner * 8 + outer, swapped)

    lax.fori_loop(0, ROWS, lookup, None)
    table[ROWS * NPER] = core
    copies[ROWS].wait()

    def convert(r, _):
        pltpu.make_async_copy(near.at[pl.ds(r * NPER, NPER)], near_v.at[pl.ds(r * NPER, NPER)], sems.at[r]).wait()
        own_ref[r] = tall(near_v[r * NPER] * near_mask[r * NPER].astype(jnp.float32))
        for s in range(NPER):
            if s < NPER - 1:
                slot = r * NPER + s + 1
                tile = near_v[slot] * near_mask[slot].astype(jnp.float32)
            else:
                tile = far_v[r] * far_mask[r].astype(jnp.float32)
            t_ref[r, s // 2, :, pl.ds((s % 2) * TB, TB)] = tall(tile)

    lax.fori_loop(0, ROWS, convert, None)


def prepare(near_tiles, near_src, near_mask, far_tiles, far_src, far_mask):
    here = jnp.stack([lax.axis_index("dom"), lax.axis_index("near")]).astype(jnp.int32)
    in_hbm = lambda x: pltpu.with_memory_space_constraint(x, pltpu.MemorySpace.HBM)
    hbm, vmem, smem = (pl.BlockSpec(memory_space=getattr(pltpu.MemorySpace, m)) for m in ("HBM", "VMEM", "SMEM"))
    return pl.pallas_call(
        prep_kernel,
        in_specs=[smem] * 5 + [hbm] * 2,
        out_specs=[vmem, vmem, smem],
        out_shape=[
            jax.ShapeDtypeStruct((ROWS, 2 * TB, TB), jnp.bfloat16),
            jax.ShapeDtypeStruct((ROWS, NPER // 2, 2 * TB, 2 * TB), jnp.bfloat16),
            jax.ShapeDtypeStruct((ROWS * NPER + 1,), jnp.int32),
        ],
        scratch_shapes=[
            pltpu.VMEM((ROWS * NPER, TB, TB), jnp.float32),
            pltpu.VMEM((ROWS, TB, TB), jnp.float32),
            pltpu.SemaphoreType.DMA((ROWS + 1,)),
        ],
        compiler_params=PARAMS,
        name="prepare",
    )(*map(in_hbm, (near_src, near_mask, far_src, far_mask)), here, in_hbm(near_tiles), in_hbm(far_tiles))


def own_kernel(coefs, t_ref, head, tail, straight, crossed, *refs):
    own, times, back = coefs
    out, v_ref = refs[-2:]
    for half, part in enumerate((head, tail)):

        def row(t, _):
            here = tile_rows(t)
            r = half * HEAD + t
            tile = part[here, :]
            v_ref[r] = wide(tile)
            value = own * tile + times * fold(dot(t_ref[r], v_ref[r], ((1,), (0,))))
            if back:
                value = value - refs[half][here, :]
            out[tile_rows(r), :] = value

        lax.fori_loop(0, HEAD, row, None)

    def neighbour(t, _):
        for b, part in enumerate((straight, crossed)):
            v_ref[ROWS + b * HEAD + t] = wide(part[tile_rows(t), :])

    lax.fori_loop(0, HEAD, neighbour, None)


def tile_rows(t):
    return pl.ds(pl.multiple_of(t * TB, TB), TB)


def call(kernel, args, outs, scratch=(), scalars=0, aliases={}):
    vmem = pl.BlockSpec(memory_space=pltpu.MemorySpace.VMEM)
    smem = pl.BlockSpec(memory_space=pltpu.MemorySpace.SMEM)
    return pl.pallas_call(
        kernel,
        in_specs=[smem] * scalars + [vmem] * (len(args) - scalars),
        out_specs=[vmem] * len(outs),
        out_shape=outs,
        scratch_shapes=list(scratch),
        input_output_aliases=aliases,
        compiler_params=PARAMS,
    )(*args)


SOURCES = jax.ShapeDtypeStruct((NEAR_BUFFERS, TB, 2 * TB), jnp.bfloat16)
BLOCK = jax.ShapeDtypeStruct((ROWS * TB, TB), jnp.float32)
PART = jax.ShapeDtypeStruct((HEAD * TB, TB), jnp.float32)
SMALL = jax.ShapeDtypeStruct((TB, TB), jnp.float32)


def apply_own(coefs, tiles, state, prev, halo):
    args = [tiles[0], *state, *halo[:2], *(prev or ())]
    return call(partial(own_kernel, (*coefs, prev is not None)), args, [BLOCK, SOURCES])


def take_relayed(v_ref, relayed):
    def step(t, _):
        v_ref[ROWS + 2 * HEAD + t] = wide(relayed[tile_rows(t), :])

    lax.fori_loop(0, HEAD, step, None)


def finished_rows(times, index, t_ref, base, v_ref, far, out, store):
    def source(r, s):
        at = index[r * NPER + s]
        if s < NPER - 1:
            return v_ref[at]
        piece = at & 7
        here = tile_rows(at >> 3 & 3)
        tile = far[4][tile_rows(at >> 3), :]
        for b in (0, 1, 2, 3, 5):
            tile = jnp.where(piece == b, far[b][here, :], tile)
        return wide(tile)

    def half(h, _):
        for t in range(STEP):
            r = h * STEP + t
            acc = None
            for p in range(NPER // 2):
                rhs = jnp.concatenate([source(r, 2 * p), source(r, 2 * p + 1)], axis=0)
                part = dot(t_ref[r, p], rhs, ((1,), (0,)))
                acc = part if acc is None else acc + part
            out[tile_rows(r), :] = store(base[tile_rows(r), :] + times * fold(acc))

    lax.fori_loop(0, ROWS // STEP, half, None)


def rest_kernel(times, carries, index, bound, t_ref, base, *refs):
    far, relayed, _ = refs[:6], *refs[6:8]
    refs = list(refs[8:])
    parts = [refs.pop(0) for _ in range(3)] + [relayed] if carries == "take" else None
    v_ref, head, tail, edge = refs[:4]
    o_ref = refs[-1]
    take_relayed(v_ref, relayed)
    finished_rows(times, index, t_ref, base, v_ref, far, o_ref, lambda row: row)
    head[pl.ds(0, HEAD * TB), :] = o_ref[pl.ds(0, HEAD * TB), :]
    tail[...] = o_ref[pl.ds(HEAD * TB, HEAD * TB), :]
    rows = lax.broadcasted_iota(jnp.int32, (TB, TB), 0)
    edge[pl.ds(0, TB), :] = jnp.where(rows < bound[0], o_ref[pl.ds(0, TB), :], 0.0)
    if carries == "give":
        both = wide(o_ref[...])
        edge[pl.ds(TB, TB), :] = fold(dot(both, both, ((0,), (0,))))
    if carries == "pass":
        head[CARRY, :] = far[2][CARRY, :] + far[5][CARRY, :]
    if carries == "take":
        mine, straight, crossed, opposite = (part[CARRY, :] for part in parts)
        refs[4][...] = (mine + opposite) + (straight + crossed)


def last_kernel(times, index, t_ref, base, *refs):
    far, relayed, block, _, v_ref, out, o_ref = refs[:6], *refs[6:]
    take_relayed(v_ref, relayed)
    finished_rows(times, index, t_ref, base, v_ref, far, o_ref, wide)
    out[pl.ds(0, TB), :] = fold(dot(wide(block[...]), o_ref[...], ((0,), (0,))))
    out[pl.ds(TB, TB), :] = far[2][CARRY, :] + far[5][CARRY, :]


CARRY = pl.ds(HEAD * TB, TB)


def tiles_of(number):
    return jax.ShapeDtypeStruct((number * TB, TB), jnp.float32)


def apply_rest(times, carries, index, bound, tiles, base, v, relayed, far, parts):
    args = [index, bound, tiles[1], base, *far, relayed, v, *(parts if carries == "take" else ())]
    head = tiles_of(HEAD + 1) if carries == "pass" else PART
    outs = [SOURCES, head, PART, tiles_of(2) if carries == "give" else SMALL]
    outs += [SMALL] if carries == "take" else []
    scratch = [pltpu.VMEM((ROWS * TB, TB), jnp.float32)]
    _, head, tail, edge, *total = call(
        partial(rest_kernel, times, carries), args, outs, scratch, scalars=2, aliases={11: 0}
    )
    return [head, tail], edge, total


def apply_last(times, index, tiles, base, v, relayed, far, block):
    args = [index, tiles[1], base, *far, relayed, block, v]
    scratch = [pltpu.VMEM((ROWS * TB, 2 * TB), jnp.bfloat16)]
    return call(
        partial(last_kernel, times), args, [SOURCES, tiles_of(2)], scratch, scalars=1,
        aliases={len(args) - 1: 0},
    )[1]


def start_kernel(bound, block, head, tail, edge):
    head[...] = block[pl.ds(0, HEAD * TB), :]
    tail[...] = block[pl.ds(HEAD * TB, HEAD * TB), :]
    rows = lax.broadcasted_iota(jnp.int32, (TB, TB), 0)
    edge[...] = jnp.where(rows < bound[0], block[pl.ds(0, TB), :], 0.0)


def start(bound, block):
    vmem = pl.BlockSpec(memory_space=pltpu.MemorySpace.VMEM)
    head = jax.ShapeDtypeStruct((HEAD * TB, TB), jnp.float32)
    return pl.pallas_call(
        start_kernel,
        in_specs=[pl.BlockSpec(memory_space=pltpu.MemorySpace.SMEM), vmem],
        out_specs=[vmem] * 3,
        out_shape=[head, head, jax.ShapeDtypeStruct((TB, TB), jnp.float32)],
        compiler_params=PARAMS,
        name="begin",
    )(bound, block)


def pack_kernel(rows, carry, *refs):
    def step(t, _):
        for i, ref in enumerate(refs[:-1]):
            refs[-1][tile_rows(i * (rows // TB) + t), :] = ref[tile_rows(t), :]

    lax.fori_loop(0, rows // TB, step, None)
    at = rows * (len(refs) - 1)
    if carry:
        mine, straight, crossed, opposite = (ref[pl.ds(rows, TB), :] for ref in refs[:-1])
        refs[-1][pl.ds(at, TB), :] = (mine + opposite) + (straight + crossed)


def pack(rows, parts, carry=False):
    out = tiles_of(len(parts) * rows // TB + carry)
    return call(partial(pack_kernel, rows, carry), parts, [out])[0]


def sum_kernel(packed, one, three, two, out):
    rows = pl.ds(0, HEAD * TB)
    out[rows, :] = three[rows, :]
    out[CARRY, :] = (packed[CARRY, :] + two[CARRY, :]) + (one[CARRY, :] + three[CARRY, :])


def times_transpose(row, inv):
    return fold(dot(tall(row), inv, ((1,), (1,))))


def norm_kernel(head, tail, inverse, edge, out, both, o_ref):
    inv = tall(inverse[...])
    for half, part in enumerate((head, tail)):

        def step(h, _):
            for t in range(STEP):
                row = times_transpose(part[tile_rows(h * STEP + t), :], inv)
                where = tile_rows(half * HEAD + h * STEP + t)
                out[where, :] = row
                o_ref[where, :] = wide(row)

        lax.fori_loop(0, HEAD // STEP, step, None)
    both[pl.ds(0, TB), :] = edge[...]
    both[pl.ds(TB, TB), :] = fold(dot(o_ref[...], o_ref[...], ((0,), (0,))))


def normalise(state, inverse, edge):
    scratch = [pltpu.VMEM((ROWS * TB, 2 * TB), jnp.bfloat16)]
    return call(norm_kernel, [*state, inverse, edge], [BLOCK, tiles_of(2)], scratch)


def thirds(x):
    high = x.astype(jnp.bfloat16).astype(jnp.float32)
    rest = x - high
    middle = rest.astype(jnp.bfloat16).astype(jnp.float32)
    return high, middle, rest - middle


def factor(gram, aug):
    rows = lax.broadcasted_iota(jnp.int32, (TB, TB), 0)
    lanes = lax.broadcasted_iota(jnp.int32, (TB, TB), 1)
    aug[:, pl.ds(0, TB)] = gram
    aug[:, pl.ds(TB, TB)] = jnp.where(rows == lanes, 1.0, 0.0)
    sub = lax.broadcasted_iota(jnp.int32, (PANEL, TB), 0)
    lane = lax.broadcasted_iota(jnp.int32, (PANEL, TB), 1)
    below = lax.broadcasted_iota(jnp.int32, (TB, 2 * TB), 0)

    def step(number, _):
        at = pl.multiple_of(number * PANEL, PANEL)
        here = pl.ds(at, PANEL)
        left = aug[here, pl.ds(0, TB)]
        right = aug[here, pl.ds(TB, TB)]
        turned = pltpu.roll(left, TB - at, 1)
        columns = [jnp.broadcast_to(turned[:, k : k + 1], (PANEL, TB)) for k in range(PANEL)]
        for i in range(PANEL):
            times = jnp.where(sub > i, columns[i], 0.0) / columns[i][i : i + 1, :]
            for k in range(i + 1, PANEL):
                columns[k] = columns[k] - times * columns[k][i : i + 1, :]
            left = left - times * left[i : i + 1, :]
            right = right - times * right[i : i + 1, :]
        pivots = jnp.sum(jnp.where(lane == sub + at, left, 0.0), axis=1, keepdims=True)
        scale = lax.rsqrt(pivots)
        scale = scale * (1.5 - 0.5 * pivots * scale * scale)
        panel = jnp.concatenate([left * scale, right * scale], axis=1)
        high, middle, low = thirds(panel)
        a = [x[:, :TB] for x in (high, high, middle, high, middle, low)]
        b = [high, middle, high, low, middle, high]
        a = jnp.concatenate(a, axis=0).astype(jnp.bfloat16)
        b = jnp.concatenate(b, axis=0).astype(jnp.bfloat16)
        update = dot(a, b, ((0,), (0,)))
        aug[...] = jnp.where(below >= at + PANEL, aug[...] - update, aug[...])
        aug[here, :] = panel

    lax.fori_loop(0, TB // PANEL, step, None)
    return aug[:, pl.ds(TB, TB)]


def factor_kernel(gram, out, aug):
    out[...] = factor(gram[...] * (1.0 / NODES), aug)


def inverse_factor(gram):
    vmem = pl.BlockSpec(memory_space=pltpu.MemorySpace.VMEM)
    return pl.pallas_call(
        factor_kernel,
        in_specs=[vmem],
        out_specs=vmem,
        out_shape=jax.ShapeDtypeStruct((TB, TB), jnp.float32),
        scratch_shapes=[pltpu.VMEM((TB, 2 * TB), jnp.float32)],
        compiler_params=PARAMS,
        name="factor",
    )(gram)


def encode_kernel(block, inverse, out):
    inv = tall(inverse[...])

    def step(h, _):
        for t in range(HEAD):
            where = tile_rows(h * HEAD + t)
            out[where, :] = times_transpose(block[where, :], inv)

    lax.fori_loop(0, ROWS // HEAD, step, None)


def rayleigh_kernel(projection, first, second, out):
    inv = tall(second[...])
    right = times_transpose(projection[...] * (1.0 / NODES), tall(first[...]))
    out[...] = times_transpose(fold(dot(inv, wide(right), ((1,), (0,)))), inv)


def relay(value, along):
    return lax.ppermute(value, AXES, pairs((0, 0, 0, along), (0, 0, 0, -along)))


def exchange(head, edge, carry):
    straight = relay(head, 1)
    first = {i: cross(edge, i, 0) for i in (2, 1, 3)}
    crossed = relay(head, -1)
    forwarded = relay(straight, 1)
    packed = pack(TB, [edge, first[1], first[3], first[2]], carry)
    second = {i: cross(packed, i, 1) for i in (2, 1, 3)}
    early = pack(HEAD * TB, [packed, second[2], second[1]])
    late = second[3]
    if carry:
        (late,) = call(sum_kernel, [packed, second[1], second[3], second[2]], [tiles_of(HEAD + 1)])
    theirs = [shift(early, dc=1), shift(late, dc=1)]
    return [straight, crossed, forwarded], [packed, second[1], late, second[2]] + theirs


def ring_sum(value, axis):
    two, one, three = (shift(value, **{"d" + axis: step}) for step in (2, 1, 3))
    return (value + two) + (one + three)


def steps(start_block, near_tiles, near_src, near_mask, far_tiles, far_src, far_mask, bound_count):
    *tiles, index = prepare(near_tiles, near_src, near_mask, far_tiles, far_src, far_mask)
    first = ((1.0 - CENTER) / HALF, -1.0 / HALF)
    later = (2.0 * first[0], 2.0 * first[1])

    *state, edge = start(bound_count, start_block)
    plan = (
        [("step", first, False), ("step", later, True), ("gram", later, True)]
        + [("step", first, False), ("step", later, True), ("step", later, True)]
        + [("last", (1.0, -1.0), False)]
    )
    carries = {3: "give", 4: "pass", 5: "take"}
    before = None
    for number, (kind, coefs, back) in enumerate(plan, 1):
        if kind == "last":
            block, edge = normalise(state, inverse, edge)
        halo, far = exchange(state[0], edge, number in (4, 7))
        base, v = apply_own(coefs, tiles, state, before if back else None, halo)
        if number == 6:
            inverse = inverse_factor(gram)
        if kind == "last":
            value = apply_last(coefs[1], index, tiles, base, v, halo[2], far, block)
        else:
            parts = [state[0], *halo[:2]]
            before = state
            state, edge, total = apply_rest(
                coefs[1], carries.get(number), index, bound_count, tiles, base, v, halo[2], far, parts
            )
            if total:
                (gram,) = total
    value = ring_sum(value, "z")
    second = inverse_factor(value[TB:])
    (encodings,) = call(encode_kernel, [block, second], [BLOCK])
    projection = value[:TB]
    projection = projection + shift(projection, dc=1)
    projection = ring_sum(ring_sum(projection, "x"), "y")
    (rayleigh,) = call(rayleigh_kernel, [projection, inverse, second], [SMALL])
    return encodings, rayleigh


def solution(mesh):
    rows = P(AXES)
    return jax.shard_map(
        steps,
        mesh=mesh,
        in_specs=(rows,) * 8,
        out_specs=(rows, P()),
        check_vma=False,
    )
```

```python
from functools import partial

import jax
import jax.numpy as jnp
from jax import lax
from jax.experimental import pallas as pl
from jax.experimental.pallas import tpu as pltpu
from jax.sharding import PartitionSpec as P


TB = 128
NPER = 6
ROWS = 8
HEAD = 4
PANEL = 16
STEP = 2
CENTER = 1.3
HALF = 0.7
NODES = 131072
AXES = ("dom", "near")
NEAR_BUFFERS = 8 + 3 * HEAD
PARAMS = pltpu.CompilerParams(vmem_limit_bytes=8 << 20)


def pairs(first, second):
    out = []
    for y in range(4):
        for x in range(4):
            for c in range(2):
                for z in range(4):
                    dy, dx, dc, dz = second if c else first
                    there = (((y + dy) % 4) * 4 + (x + dx) % 4) * 2 + (c + dc) % 2
                    out.append((((y * 4 + x) * 2 + c) * 4 + z, there * 4 + (z + dz) % 4))
    return out


def shift(value, dy=0, dx=0, dc=0, dz=0):
    step = (dy, dx, dc, dz)
    return lax.ppermute(value, AXES, pairs(step, step))


def cross(value, along, stage):
    steps = ((0, along, 0, 0), (along, 0, 0, 0))
    return lax.ppermute(value, AXES, pairs(steps[stage], steps[1 - stage]))


def split(x):
    hi = x.astype(jnp.bfloat16)
    lo = (x - hi.astype(jnp.float32)).astype(jnp.bfloat16)
    return hi, lo


def wide(x):
    return jnp.concatenate(split(x), axis=1)


def tall(x):
    return jnp.concatenate(split(x), axis=0)


def fold(acc):
    return (acc[:TB, :TB] + acc[TB:, TB:]) + (acc[:TB, TB:] + acc[TB:, :TB])


def dot(a, b, dims):
    return lax.dot_general(a, b, (dims, ((), ())), preferred_element_type=jnp.float32)


def prep_kernel(near_src, near_mask, far_src, far_mask, here, near, far, own_ref, t_ref, table, near_v, far_v, sems):
    dom, z = here[0], here[1]
    core = dom & 1
    copies = [
        pltpu.make_async_copy(near.at[pl.ds(r * NPER, NPER)], near_v.at[pl.ds(r * NPER, NPER)], sems.at[r])
        for r in range(ROWS)
    ]
    copies.append(pltpu.make_async_copy(far, far_v, sems.at[ROWS]))
    for copy in copies:
        copy.start()

    def lookup(r, _):
        for s in range(NPER):
            if s < NPER - 1:
                source = near_src[r * NPER + s + 1]
                away = ((source >> 3) - z) & 3
                straight = jnp.where(core == 0, 3, 1)
                buffer = jnp.where(away == 2, 2, jnp.where(away == straight, 0, 1))
                halo = ROWS + buffer * HEAD + (source & 3)
                table[r * NPER + s] = jnp.where(away == 0, source & 7, halo)
            else:
                chip = far_src[r] >> 1
                dy = (0x78 >> 2 * (((chip >> 2) - (dom >> 3)) & 3)) & 3
                dx = (0x78 >> 2 * ((chip - (dom >> 1)) & 3)) & 3
                theirs = far_src[r] & 1
                inner = jnp.where(theirs == 0, dx, dy)
                outer = jnp.where(theirs == 0, dy, dx)
                piece = jnp.where(outer == 0, 0, jnp.where(outer == 3, 4, 8))
                swapped = jnp.where(outer == 1, inner * 8 + 5, (piece + inner) * 8 + 4)
                table[r * NPER + s] = jnp.where(theirs == core, inner * 8 + outer, swapped)

    lax.fori_loop(0, ROWS, lookup, None)
    table[ROWS * NPER] = core
    copies[ROWS].wait()

    def convert(r, _):
        pltpu.make_async_copy(near.at[pl.ds(r * NPER, NPER)], near_v.at[pl.ds(r * NPER, NPER)], sems.at[r]).wait()
        own_ref[r] = tall(near_v[r * NPER] * near_mask[r * NPER].astype(jnp.float32))
        for s in range(NPER):
            if s < NPER - 1:
                slot = r * NPER + s + 1
                tile = near_v[slot] * near_mask[slot].astype(jnp.float32)
            else:
                tile = far_v[r] * far_mask[r].astype(jnp.float32)
            t_ref[r, s // 2, :, pl.ds((s % 2) * TB, TB)] = tall(tile)

    lax.fori_loop(0, ROWS, convert, None)


def prepare(near_tiles, near_src, near_mask, far_tiles, far_src, far_mask):
    here = jnp.stack([lax.axis_index("dom"), lax.axis_index("near")]).astype(jnp.int32)
    in_hbm = lambda x: pltpu.with_memory_space_constraint(x, pltpu.MemorySpace.HBM)
    hbm, vmem, smem = (pl.BlockSpec(memory_space=getattr(pltpu.MemorySpace, m)) for m in ("HBM", "VMEM", "SMEM"))
    return pl.pallas_call(
        prep_kernel,
        in_specs=[smem] * 5 + [hbm] * 2,
        out_specs=[vmem, vmem, smem],
        out_shape=[
            jax.ShapeDtypeStruct((ROWS, 2 * TB, TB), jnp.bfloat16),
            jax.ShapeDtypeStruct((ROWS, NPER // 2, 2 * TB, 2 * TB), jnp.bfloat16),
            jax.ShapeDtypeStruct((ROWS * NPER + 1,), jnp.int32),
        ],
        scratch_shapes=[
            pltpu.VMEM((ROWS * NPER, TB, TB), jnp.float32),
            pltpu.VMEM((ROWS, TB, TB), jnp.float32),
            pltpu.SemaphoreType.DMA((ROWS + 1,)),
        ],
        compiler_params=PARAMS,
        name="prepare",
    )(*map(in_hbm, (near_src, near_mask, far_src, far_mask)), here, in_hbm(near_tiles), in_hbm(far_tiles))


def own_kernel(coefs, t_ref, head, tail, straight, crossed, *refs):
    own, times, back = coefs
    out, v_ref = refs[-2:]
    for half, part in enumerate((head, tail)):

        def row(t, _):
            here = tile_rows(t)
            r = half * HEAD + t
            tile = part[here, :]
            v_ref[r] = wide(tile)
            value = own * tile + times * fold(dot(t_ref[r], v_ref[r], ((1,), (0,))))
            if back:
                value = value - refs[half][here, :]
            out[tile_rows(r), :] = value

        lax.fori_loop(0, HEAD, row, None)

    def neighbour(t, _):
        for b, part in enumerate((straight, crossed)):
            v_ref[ROWS + b * HEAD + t] = wide(part[tile_rows(t), :])

    lax.fori_loop(0, HEAD, neighbour, None)


def tile_rows(t):
    return pl.ds(pl.multiple_of(t * TB, TB), TB)


def call(kernel, args, outs, scratch=(), scalars=0, aliases={}):
    vmem = pl.BlockSpec(memory_space=pltpu.MemorySpace.VMEM)
    smem = pl.BlockSpec(memory_space=pltpu.MemorySpace.SMEM)
    return pl.pallas_call(
        kernel,
        in_specs=[smem] * scalars + [vmem] * (len(args) - scalars),
        out_specs=[vmem] * len(outs),
        out_shape=outs,
        scratch_shapes=list(scratch),
        input_output_aliases=aliases,
        compiler_params=PARAMS,
    )(*args)


SOURCES = jax.ShapeDtypeStruct((NEAR_BUFFERS, TB, 2 * TB), jnp.bfloat16)
BLOCK = jax.ShapeDtypeStruct((ROWS * TB, TB), jnp.float32)
PART = jax.ShapeDtypeStruct((HEAD * TB, TB), jnp.float32)
SMALL = jax.ShapeDtypeStruct((TB, TB), jnp.float32)


def apply_own(coefs, tiles, state, prev, halo):
    args = [tiles[0], *state, *halo[:2], *(prev or ())]
    return call(partial(own_kernel, (*coefs, prev is not None)), args, [BLOCK, SOURCES])


def take_relayed(v_ref, relayed):
    def step(t, _):
        v_ref[ROWS + 2 * HEAD + t] = wide(relayed[tile_rows(t), :])

    lax.fori_loop(0, HEAD, step, None)


def finished_rows(times, index, t_ref, base, v_ref, far, out, store):
    def source(r, s):
        at = index[r * NPER + s]
        if s < NPER - 1:
            return v_ref[at]
        piece = at & 7
        here = tile_rows(at >> 3 & 3)
        tile = far[4][tile_rows(at >> 3), :]
        for b in (0, 1, 2, 3, 5):
            tile = jnp.where(piece == b, far[b][here, :], tile)
        return wide(tile)

    def half(h, _):
        for t in range(STEP):
            r = h * STEP + t
            acc = None
            for p in range(NPER // 2):
                rhs = jnp.concatenate([source(r, 2 * p), source(r, 2 * p + 1)], axis=0)
                part = dot(t_ref[r, p], rhs, ((1,), (0,)))
                acc = part if acc is None else acc + part
            out[tile_rows(r), :] = store(base[tile_rows(r), :] + times * fold(acc))

    lax.fori_loop(0, ROWS // STEP, half, None)


def rest_kernel(times, carries, index, bound, t_ref, base, *refs):
    far, relayed, _ = refs[:6], *refs[6:8]
    refs = list(refs[8:])
    parts = [refs.pop(0) for _ in range(3)] + [relayed] if carries == "take" else None
    v_ref, head, tail, edge = refs[:4]
    o_ref = refs[-1]
    take_relayed(v_ref, relayed)
    finished_rows(times, index, t_ref, base, v_ref, far, o_ref, lambda row: row)
    head[pl.ds(0, HEAD * TB), :] = o_ref[pl.ds(0, HEAD * TB), :]
    tail[...] = o_ref[pl.ds(HEAD * TB, HEAD * TB), :]
    rows = lax.broadcasted_iota(jnp.int32, (TB, TB), 0)
    edge[pl.ds(0, TB), :] = jnp.where(rows < bound[0], o_ref[pl.ds(0, TB), :], 0.0)
    if carries == "give":
        both = wide(o_ref[...])
        edge[pl.ds(TB, TB), :] = fold(dot(both, both, ((0,), (0,))))
    if carries == "pass":
        head[CARRY, :] = far[1][CARRY, :] + far[5][CARRY, :]
    if carries == "take":
        mine, straight, crossed, opposite = (part[CARRY, :] for part in parts)
        refs[4][...] = (mine + opposite) + (straight + crossed)


def last_kernel(times, index, t_ref, base, *refs):
    far, relayed, block, _, v_ref, out, o_ref = refs[:6], *refs[6:]
    take_relayed(v_ref, relayed)
    finished_rows(times, index, t_ref, base, v_ref, far, o_ref, wide)
    out[pl.ds(0, TB), :] = fold(dot(wide(block[...]), o_ref[...], ((0,), (0,))))
    out[pl.ds(TB, TB), :] = far[1][CARRY, :] + far[5][CARRY, :]


CARRY = pl.ds(HEAD * TB, TB)


def tiles_of(number):
    return jax.ShapeDtypeStruct((number * TB, TB), jnp.float32)


def apply_rest(times, carries, index, bound, tiles, base, v, relayed, far, parts):
    args = [index, bound, tiles[1], base, *far, relayed, v, *(parts if carries == "take" else ())]
    head = tiles_of(HEAD + 1) if carries == "pass" else PART
    outs = [SOURCES, head, PART, tiles_of(2) if carries == "give" else SMALL]
    outs += [SMALL] if carries == "take" else []
    scratch = [pltpu.VMEM((ROWS * TB, TB), jnp.float32)]
    _, head, tail, edge, *total = call(
        partial(rest_kernel, times, carries), args, outs, scratch, scalars=2, aliases={11: 0}
    )
    return [head, tail], edge, total


def apply_last(times, index, tiles, base, v, relayed, far, block):
    args = [index, tiles[1], base, *far, relayed, block, v]
    scratch = [pltpu.VMEM((ROWS * TB, 2 * TB), jnp.bfloat16)]
    return call(
        partial(last_kernel, times), args, [SOURCES, tiles_of(2)], scratch, scalars=1,
        aliases={len(args) - 1: 0},
    )[1]


def start_kernel(bound, block, head, tail, edge):
    head[...] = block[pl.ds(0, HEAD * TB), :]
    tail[...] = block[pl.ds(HEAD * TB, HEAD * TB), :]
    rows = lax.broadcasted_iota(jnp.int32, (TB, TB), 0)
    edge[...] = jnp.where(rows < bound[0], block[pl.ds(0, TB), :], 0.0)


def start(bound, block):
    vmem = pl.BlockSpec(memory_space=pltpu.MemorySpace.VMEM)
    head = jax.ShapeDtypeStruct((HEAD * TB, TB), jnp.float32)
    return pl.pallas_call(
        start_kernel,
        in_specs=[pl.BlockSpec(memory_space=pltpu.MemorySpace.SMEM), vmem],
        out_specs=[vmem] * 3,
        out_shape=[head, head, jax.ShapeDtypeStruct((TB, TB), jnp.float32)],
        compiler_params=PARAMS,
        name="begin",
    )(bound, block)


def pack_kernel(rows, carry, *refs):
    def step(t, _):
        for i, ref in enumerate(refs[:-1]):
            refs[-1][tile_rows(i * (rows // TB) + t), :] = ref[tile_rows(t), :]

    lax.fori_loop(0, rows // TB, step, None)
    at = rows * (len(refs) - 1)
    if carry:
        mine, straight, crossed, opposite = (ref[pl.ds(rows, TB), :] for ref in refs[:-1])
        refs[-1][pl.ds(at, TB), :] = (mine + opposite) + (straight + crossed)


def pack(rows, parts, carry=False):
    out = tiles_of(len(parts) * rows // TB + carry)
    return call(partial(pack_kernel, rows, carry), parts, [out])[0]


def sum_kernel(packed, one, three, two, out):
    rows = pl.ds(0, HEAD * TB)
    out[rows, :] = one[rows, :]
    out[CARRY, :] = (packed[CARRY, :] + two[CARRY, :]) + (one[CARRY, :] + three[CARRY, :])


def times_transpose(row, inv):
    return fold(dot(tall(row), inv, ((1,), (1,))))


def norm_kernel(head, tail, inverse, edge, out, both, o_ref):
    inv = tall(inverse[...])
    for half, part in enumerate((head, tail)):

        def step(h, _):
            for t in range(STEP):
                row = times_transpose(part[tile_rows(h * STEP + t), :], inv)
                where = tile_rows(half * HEAD + h * STEP + t)
                out[where, :] = row
                o_ref[where, :] = wide(row)

        lax.fori_loop(0, HEAD // STEP, step, None)
    both[pl.ds(0, TB), :] = edge[...]
    both[pl.ds(TB, TB), :] = fold(dot(o_ref[...], o_ref[...], ((0,), (0,))))


def normalise(state, inverse, edge):
    scratch = [pltpu.VMEM((ROWS * TB, 2 * TB), jnp.bfloat16)]
    return call(norm_kernel, [*state, inverse, edge], [BLOCK, tiles_of(2)], scratch)


def thirds(x):
    high = x.astype(jnp.bfloat16).astype(jnp.float32)
    rest = x - high
    middle = rest.astype(jnp.bfloat16).astype(jnp.float32)
    return high, middle, rest - middle


def factor(gram, aug):
    rows = lax.broadcasted_iota(jnp.int32, (TB, TB), 0)
    lanes = lax.broadcasted_iota(jnp.int32, (TB, TB), 1)
    aug[:, pl.ds(0, TB)] = gram
    aug[:, pl.ds(TB, TB)] = jnp.where(rows == lanes, 1.0, 0.0)
    sub = lax.broadcasted_iota(jnp.int32, (PANEL, TB), 0)
    lane = lax.broadcasted_iota(jnp.int32, (PANEL, TB), 1)
    below = lax.broadcasted_iota(jnp.int32, (TB, 2 * TB), 0)

    def step(number, _):
        at = pl.multiple_of(number * PANEL, PANEL)
        here = pl.ds(at, PANEL)
        left = aug[here, pl.ds(0, TB)]
        right = aug[here, pl.ds(TB, TB)]
        turned = pltpu.roll(left, TB - at, 1)
        columns = [jnp.broadcast_to(turned[:, k : k + 1], (PANEL, TB)) for k in range(PANEL)]
        for i in range(PANEL):
            times = jnp.where(sub > i, columns[i], 0.0) / columns[i][i : i + 1, :]
            for k in range(i + 1, PANEL):
                columns[k] = columns[k] - times * columns[k][i : i + 1, :]
            left = left - times * left[i : i + 1, :]
            right = right - times * right[i : i + 1, :]
        pivots = jnp.sum(jnp.where(lane == sub + at, left, 0.0), axis=1, keepdims=True)
        scale = lax.rsqrt(pivots)
        scale = scale * (1.5 - 0.5 * pivots * scale * scale)
        panel = jnp.concatenate([left * scale, right * scale], axis=1)
        high, middle, low = thirds(panel)
        a = [x[:, :TB] for x in (high, high, middle, high, middle, low)]
        b = [high, middle, high, low, middle, high]
        a = jnp.concatenate(a, axis=0).astype(jnp.bfloat16)
        b = jnp.concatenate(b, axis=0).astype(jnp.bfloat16)
        update = dot(a, b, ((0,), (0,)))
        aug[...] = jnp.where(below >= at + PANEL, aug[...] - update, aug[...])
        aug[here, :] = panel

    lax.fori_loop(0, TB // PANEL, step, None)
    return aug[:, pl.ds(TB, TB)]


def factor_kernel(gram, out, aug):
    out[...] = factor(gram[...] * (1.0 / NODES), aug)


def inverse_factor(gram):
    vmem = pl.BlockSpec(memory_space=pltpu.MemorySpace.VMEM)
    return pl.pallas_call(
        factor_kernel,
        in_specs=[vmem],
        out_specs=vmem,
        out_shape=jax.ShapeDtypeStruct((TB, TB), jnp.float32),
        scratch_shapes=[pltpu.VMEM((TB, 2 * TB), jnp.float32)],
        compiler_params=PARAMS,
        name="factor",
    )(gram)


def encode_kernel(block, inverse, out):
    inv = tall(inverse[...])

    def step(h, _):
        for t in range(HEAD):
            where = tile_rows(h * HEAD + t)
            out[where, :] = times_transpose(block[where, :], inv)

    lax.fori_loop(0, ROWS // HEAD, step, None)


def rayleigh_kernel(projection, first, second, out):
    inv = tall(second[...])
    right = times_transpose(projection[...] * (1.0 / NODES), tall(first[...]))
    out[...] = times_transpose(fold(dot(inv, wide(right), ((1,), (0,)))), inv)


def relay(value, along):
    return lax.ppermute(value, AXES, pairs((0, 0, 0, along), (0, 0, 0, -along)))


def exchange(head, edge, carry):
    straight = relay(head, 1)
    first = {i: cross(edge, i, 0) for i in (2, 1, 3)}
    crossed = relay(head, -1)
    forwarded = relay(straight, 1)
    packed = pack(TB, [edge, first[1], first[3], first[2]], carry)
    second = {i: cross(packed, i, 1) for i in (2, 1, 3)}
    early = pack(HEAD * TB, [packed, second[2], second[3]])
    late = second[1]
    if carry:
        (late,) = call(sum_kernel, [packed, second[1], second[3], second[2]], [tiles_of(HEAD + 1)])
    theirs = [shift(early, dc=1), shift(late, dc=1)]
    return [straight, crossed, forwarded], [packed, late, second[3], second[2]] + theirs


def ring_sum(value, axis):
    two, one, three = (shift(value, **{"d" + axis: step}) for step in (2, 1, 3))
    return (value + two) + (one + three)


def steps(start_block, near_tiles, near_src, near_mask, far_tiles, far_src, far_mask, bound_count):
    *tiles, index = prepare(near_tiles, near_src, near_mask, far_tiles, far_src, far_mask)
    first = ((1.0 - CENTER) / HALF, -1.0 / HALF)
    later = (2.0 * first[0], 2.0 * first[1])

    *state, edge = start(bound_count, start_block)
    plan = (
        [("step", first, False), ("step", later, True), ("gram", later, True)]
        + [("step", first, False), ("step", later, True), ("step", later, True)]
        + [("last", (1.0, -1.0), False)]
    )
    carries = {3: "give", 4: "pass", 5: "take"}
    before = None
    for number, (kind, coefs, back) in enumerate(plan, 1):
        if kind == "last":
            block, edge = normalise(state, inverse, edge)
        halo, far = exchange(state[0], edge, number in (4, 7))
        base, v = apply_own(coefs, tiles, state, before if back else None, halo)
        if number == 6:
            inverse = inverse_factor(gram)
        if kind == "last":
            value = apply_last(coefs[1], index, tiles, base, v, halo[2], far, block)
        else:
            parts = [state[0], *halo[:2]]
            before = state
            state, edge, total = apply_rest(
                coefs[1], carries.get(number), index, bound_count, tiles, base, v, halo[2], far, parts
            )
            if total:
                (gram,) = total
    value = ring_sum(value, "z")
    second = inverse_factor(value[TB:])
    (encodings,) = call(encode_kernel, [block, second], [BLOCK])
    projection = value[:TB]
    projection = projection + shift(projection, dc=1)
    projection = ring_sum(ring_sum(projection, "x"), "y")
    (rayleigh,) = call(rayleigh_kernel, [projection, inverse, second], [SMALL])
    return encodings, rayleigh


def solution(mesh):
    rows = P(AXES)
    return jax.shard_map(
        steps,
        mesh=mesh,
        in_specs=(rows,) * 8,
        out_specs=(rows, P()),
        check_vma=False,
    )
```

```python
from functools import partial

import jax
import jax.numpy as jnp
from jax import lax
from jax.experimental import pallas as pl
from jax.experimental.pallas import tpu as pltpu
from jax.sharding import PartitionSpec as P


TB = 128
NPER = 6
ROWS = 8
HEAD = 4
PANEL = 16
STEP = 2
CENTER = 1.3
HALF = 0.7
NODES = 131072
AXES = ("dom", "near")
NEAR_BUFFERS = 8 + 3 * HEAD
PARAMS = pltpu.CompilerParams(vmem_limit_bytes=8 << 20)


def pairs(first, second):
    out = []
    for y in range(4):
        for x in range(4):
            for c in range(2):
                for z in range(4):
                    dy, dx, dc, dz = second if c else first
                    there = (((y + dy) % 4) * 4 + (x + dx) % 4) * 2 + (c + dc) % 2
                    out.append((((y * 4 + x) * 2 + c) * 4 + z, there * 4 + (z + dz) % 4))
    return out


def shift(value, dy=0, dx=0, dc=0, dz=0):
    step = (dy, dx, dc, dz)
    return lax.ppermute(value, AXES, pairs(step, step))


def cross(value, along, stage):
    steps = ((0, along, 0, 0), (along, 0, 0, 0))
    return lax.ppermute(value, AXES, pairs(steps[stage], steps[1 - stage]))


def split(x):
    hi = x.astype(jnp.bfloat16)
    lo = (x - hi.astype(jnp.float32)).astype(jnp.bfloat16)
    return hi, lo


def wide(x):
    return jnp.concatenate(split(x), axis=1)


def tall(x):
    return jnp.concatenate(split(x), axis=0)


def fold(acc):
    return (acc[:TB, :TB] + acc[TB:, TB:]) + (acc[:TB, TB:] + acc[TB:, :TB])


def dot(a, b, dims):
    return lax.dot_general(a, b, (dims, ((), ())), preferred_element_type=jnp.float32)


def prep_kernel(near_src, near_mask, far_src, far_mask, here, near, far, own_ref, t_ref, table, near_v, far_v, sems):
    dom, z = here[0], here[1]
    core = dom & 1
    copies = [
        pltpu.make_async_copy(near.at[pl.ds(r * NPER, NPER)], near_v.at[pl.ds(r * NPER, NPER)], sems.at[r])
        for r in range(ROWS)
    ]
    copies.append(pltpu.make_async_copy(far, far_v, sems.at[ROWS]))
    for copy in copies:
        copy.start()

    def lookup(r, _):
        for s in range(NPER):
            if s < NPER - 1:
                source = near_src[r * NPER + s + 1]
                away = ((source >> 3) - z) & 3
                straight = jnp.where(core == 0, 3, 1)
                buffer = jnp.where(away == 2, 2, jnp.where(away == straight, 0, 1))
                halo = ROWS + buffer * HEAD + (source & 3)
                table[r * NPER + s] = jnp.where(away == 0, source & 7, halo)
            else:
                chip = far_src[r] >> 1
                dy = (0x78 >> 2 * (((chip >> 2) - (dom >> 3)) & 3)) & 3
                dx = (0x78 >> 2 * ((chip - (dom >> 1)) & 3)) & 3
                theirs = far_src[r] & 1
                inner = jnp.where(theirs == 0, dx, dy)
                outer = jnp.where(theirs == 0, dy, dx)
                piece = jnp.where(outer == 0, 0, jnp.where(outer == 3, 4, 8))
                swapped = jnp.where(outer == 1, inner * 8 + 5, (piece + inner) * 8 + 4)
                table[r * NPER + s] = jnp.where(theirs == core, inner * 8 + outer, swapped)

    lax.fori_loop(0, ROWS, lookup, None)
    table[ROWS * NPER] = core
    copies[ROWS].wait()

    def convert(r, _):
        pltpu.make_async_copy(near.at[pl.ds(r * NPER, NPER)], near_v.at[pl.ds(r * NPER, NPER)], sems.at[r]).wait()
        own_ref[r] = tall(near_v[r * NPER] * near_mask[r * NPER].astype(jnp.float32))
        for s in range(NPER):
            if s < NPER - 1:
                slot = r * NPER + s + 1
                tile = near_v[slot] * near_mask[slot].astype(jnp.float32)
            else:
                tile = far_v[r] * far_mask[r].astype(jnp.float32)
            t_ref[r, :, pl.ds(s * TB, TB)] = tall(tile)

    lax.fori_loop(0, ROWS, convert, None)


def prepare(near_tiles, near_src, near_mask, far_tiles, far_src, far_mask):
    here = jnp.stack([lax.axis_index("dom"), lax.axis_index("near")]).astype(jnp.int32)
    in_hbm = lambda x: pltpu.with_memory_space_constraint(x, pltpu.MemorySpace.HBM)
    hbm, vmem, smem = (pl.BlockSpec(memory_space=getattr(pltpu.MemorySpace, m)) for m in ("HBM", "VMEM", "SMEM"))
    return pl.pallas_call(
        prep_kernel,
        in_specs=[smem] * 5 + [hbm] * 2,
        out_specs=[vmem, vmem, smem],
        out_shape=[
            jax.ShapeDtypeStruct((ROWS, 2 * TB, TB), jnp.bfloat16),
            jax.ShapeDtypeStruct((ROWS, 2 * TB, NPER * TB), jnp.bfloat16),
            jax.ShapeDtypeStruct((ROWS * NPER + 1,), jnp.int32),
        ],
        scratch_shapes=[
            pltpu.VMEM((ROWS * NPER, TB, TB), jnp.float32),
            pltpu.VMEM((ROWS, TB, TB), jnp.float32),
            pltpu.SemaphoreType.DMA((ROWS + 1,)),
        ],
        compiler_params=PARAMS,
        name="prepare",
    )(*map(in_hbm, (near_src, near_mask, far_src, far_mask)), here, in_hbm(near_tiles), in_hbm(far_tiles))


def own_kernel(coefs, t_ref, head, tail, straight, crossed, *refs):
    own, times, back = coefs
    out, v_ref = refs[-2:]
    for half, part in enumerate((head, tail)):

        def row(t, _):
            here = tile_rows(t)
            r = half * HEAD + t
            tile = part[here, :]
            v_ref[r] = wide(tile)
            value = own * tile + times * fold(dot(t_ref[r], v_ref[r], ((1,), (0,))))
            if back:
                value = value - refs[half][here, :]
            out[tile_rows(r), :] = value

        lax.fori_loop(0, HEAD, row, None)

    def neighbour(t, _):
        for b, part in enumerate((straight, crossed)):
            v_ref[ROWS + b * HEAD + t] = wide(part[tile_rows(t), :])

    lax.fori_loop(0, HEAD, neighbour, None)


def tile_rows(t):
    return pl.ds(pl.multiple_of(t * TB, TB), TB)


def call(kernel, args, outs, scratch=(), scalars=0, aliases={}):
    vmem = pl.BlockSpec(memory_space=pltpu.MemorySpace.VMEM)
    smem = pl.BlockSpec(memory_space=pltpu.MemorySpace.SMEM)
    return pl.pallas_call(
        kernel,
        in_specs=[smem] * scalars + [vmem] * (len(args) - scalars),
        out_specs=[vmem] * len(outs),
        out_shape=outs,
        scratch_shapes=list(scratch),
        input_output_aliases=aliases,
        compiler_params=PARAMS,
    )(*args)


SOURCES = jax.ShapeDtypeStruct((NEAR_BUFFERS, TB, 2 * TB), jnp.bfloat16)
BLOCK = jax.ShapeDtypeStruct((ROWS * TB, TB), jnp.float32)
PART = jax.ShapeDtypeStruct((HEAD * TB, TB), jnp.float32)
SMALL = jax.ShapeDtypeStruct((TB, TB), jnp.float32)


def apply_own(coefs, tiles, state, prev, halo):
    args = [tiles[0], *state, *halo[:2], *(prev or ())]
    return call(partial(own_kernel, (*coefs, prev is not None)), args, [BLOCK, SOURCES])


def take_relayed(v_ref, relayed):
    def step(t, _):
        v_ref[ROWS + 2 * HEAD + t] = wide(relayed[tile_rows(t), :])

    lax.fori_loop(0, HEAD, step, None)


def finished_rows(times, index, t_ref, base, v_ref, far, out, store):
    def source(r, s):
        at = index[r * NPER + s]
        if s < NPER - 1:
            return v_ref[at]
        piece = at & 7
        here = tile_rows(at >> 3 & 3)
        tile = far[4][tile_rows(at >> 3), :]
        for b in (0, 1, 2, 3, 5):
            tile = jnp.where(piece == b, far[b][here, :], tile)
        return wide(tile)

    def half(h, _):
        for t in range(STEP):
            r = h * STEP + t
            acc = dot(t_ref[r], jnp.concatenate([source(r, s) for s in range(NPER)], axis=0), ((1,), (0,)))
            out[tile_rows(r), :] = store(base[tile_rows(r), :] + times * fold(acc))

    lax.fori_loop(0, ROWS // STEP, half, None)


def rest_kernel(times, carries, index, bound, t_ref, base, *refs):
    far, relayed, _ = refs[:6], *refs[6:8]
    refs = list(refs[8:])
    parts = [refs.pop(0) for _ in range(3)] + [relayed] if carries == "take" else None
    v_ref, head, tail, edge = refs[:4]
    o_ref = refs[-1]
    take_relayed(v_ref, relayed)
    finished_rows(times, index, t_ref, base, v_ref, far, o_ref, lambda row: row)
    head[pl.ds(0, HEAD * TB), :] = o_ref[pl.ds(0, HEAD * TB), :]
    tail[...] = o_ref[pl.ds(HEAD * TB, HEAD * TB), :]
    rows = lax.broadcasted_iota(jnp.int32, (TB, TB), 0)
    edge[pl.ds(0, TB), :] = jnp.where(rows < bound[0], o_ref[pl.ds(0, TB), :], 0.0)
    if carries == "give":
        both = wide(o_ref[...])
        edge[pl.ds(TB, TB), :] = fold(dot(both, both, ((0,), (0,))))
    if carries == "pass":
        head[CARRY, :] = far[1][CARRY, :] + far[5][CARRY, :]
    if carries == "take":
        mine, straight, crossed, opposite = (part[CARRY, :] for part in parts)
        refs[4][...] = (mine + opposite) + (straight + crossed)


def last_kernel(times, index, t_ref, base, *refs):
    far, relayed, block, _, v_ref, out, o_ref = refs[:6], *refs[6:]
    take_relayed(v_ref, relayed)
    finished_rows(times, index, t_ref, base, v_ref, far, o_ref, wide)
    out[pl.ds(0, TB), :] = fold(dot(wide(block[...]), o_ref[...], ((0,), (0,))))
    out[pl.ds(TB, TB), :] = far[1][CARRY, :] + far[5][CARRY, :]


CARRY = pl.ds(HEAD * TB, TB)


def tiles_of(number):
    return jax.ShapeDtypeStruct((number * TB, TB), jnp.float32)


def apply_rest(times, carries, index, bound, tiles, base, v, relayed, far, parts):
    args = [index, bound, tiles[1], base, *far, relayed, v, *(parts if carries == "take" else ())]
    head = tiles_of(HEAD + 1) if carries == "pass" else PART
    outs = [SOURCES, head, PART, tiles_of(2) if carries == "give" else SMALL]
    outs += [SMALL] if carries == "take" else []
    scratch = [pltpu.VMEM((ROWS * TB, TB), jnp.float32)]
    _, head, tail, edge, *total = call(
        partial(rest_kernel, times, carries), args, outs, scratch, scalars=2, aliases={11: 0}
    )
    return [head, tail], edge, total


def apply_last(times, index, tiles, base, v, relayed, far, block):
    args = [index, tiles[1], base, *far, relayed, block, v]
    scratch = [pltpu.VMEM((ROWS * TB, 2 * TB), jnp.bfloat16)]
    return call(
        partial(last_kernel, times), args, [SOURCES, tiles_of(2)], scratch, scalars=1,
        aliases={len(args) - 1: 0},
    )[1]


def start_kernel(bound, block, head, tail, edge):
    head[...] = block[pl.ds(0, HEAD * TB), :]
    tail[...] = block[pl.ds(HEAD * TB, HEAD * TB), :]
    rows = lax.broadcasted_iota(jnp.int32, (TB, TB), 0)
    edge[...] = jnp.where(rows < bound[0], block[pl.ds(0, TB), :], 0.0)


def start(bound, block):
    vmem = pl.BlockSpec(memory_space=pltpu.MemorySpace.VMEM)
    head = jax.ShapeDtypeStruct((HEAD * TB, TB), jnp.float32)
    return pl.pallas_call(
        start_kernel,
        in_specs=[pl.BlockSpec(memory_space=pltpu.MemorySpace.SMEM), vmem],
        out_specs=[vmem] * 3,
        out_shape=[head, head, jax.ShapeDtypeStruct((TB, TB), jnp.float32)],
        compiler_params=PARAMS,
        name="begin",
    )(bound, block)


def pack_kernel(rows, carry, *refs):
    def step(t, _):
        for i, ref in enumerate(refs[:-1]):
            refs[-1][tile_rows(i * (rows // TB) + t), :] = ref[tile_rows(t), :]

    lax.fori_loop(0, rows // TB, step, None)
    at = rows * (len(refs) - 1)
    if carry:
        mine, straight, crossed, opposite = (ref[pl.ds(rows, TB), :] for ref in refs[:-1])
        refs[-1][pl.ds(at, TB), :] = (mine + opposite) + (straight + crossed)


def pack(rows, parts, carry=False):
    out = tiles_of(len(parts) * rows // TB + carry)
    return call(partial(pack_kernel, rows, carry), parts, [out])[0]


def sum_kernel(packed, one, three, two, out):
    rows = pl.ds(0, HEAD * TB)
    out[rows, :] = one[rows, :]
    out[CARRY, :] = (packed[CARRY, :] + two[CARRY, :]) + (one[CARRY, :] + three[CARRY, :])


def times_transpose(row, inv):
    return fold(dot(tall(row), inv, ((1,), (1,))))


def norm_kernel(head, tail, inverse, edge, out, both, o_ref):
    inv = tall(inverse[...])
    for half, part in enumerate((head, tail)):

        def step(h, _):
            for t in range(STEP):
                row = times_transpose(part[tile_rows(h * STEP + t), :], inv)
                where = tile_rows(half * HEAD + h * STEP + t)
                out[where, :] = row
                o_ref[where, :] = wide(row)

        lax.fori_loop(0, HEAD // STEP, step, None)
    both[pl.ds(0, TB), :] = edge[...]
    both[pl.ds(TB, TB), :] = fold(dot(o_ref[...], o_ref[...], ((0,), (0,))))


def normalise(state, inverse, edge):
    scratch = [pltpu.VMEM((ROWS * TB, 2 * TB), jnp.bfloat16)]
    return call(norm_kernel, [*state, inverse, edge], [BLOCK, tiles_of(2)], scratch)


def thirds(x):
    high = x.astype(jnp.bfloat16).astype(jnp.float32)
    rest = x - high
    middle = rest.astype(jnp.bfloat16).astype(jnp.float32)
    return high, middle, rest - middle


def factor(gram, aug):
    rows = lax.broadcasted_iota(jnp.int32, (TB, TB), 0)
    lanes = lax.broadcasted_iota(jnp.int32, (TB, TB), 1)
    aug[:, pl.ds(0, TB)] = gram
    aug[:, pl.ds(TB, TB)] = jnp.where(rows == lanes, 1.0, 0.0)
    sub = lax.broadcasted_iota(jnp.int32, (PANEL, TB), 0)
    lane = lax.broadcasted_iota(jnp.int32, (PANEL, TB), 1)
    below = lax.broadcasted_iota(jnp.int32, (TB, 2 * TB), 0)

    def step(number, _):
        at = pl.multiple_of(number * PANEL, PANEL)
        here = pl.ds(at, PANEL)
        left = aug[here, pl.ds(0, TB)]
        right = aug[here, pl.ds(TB, TB)]
        turned = pltpu.roll(left, TB - at, 1)
        columns = [jnp.broadcast_to(turned[:, k : k + 1], (PANEL, TB)) for k in range(PANEL)]
        for i in range(PANEL):
            times = jnp.where(sub > i, columns[i], 0.0) / columns[i][i : i + 1, :]
            for k in range(i + 1, PANEL):
                columns[k] = columns[k] - times * columns[k][i : i + 1, :]
            left = left - times * left[i : i + 1, :]
            right = right - times * right[i : i + 1, :]
        pivots = jnp.sum(jnp.where(lane == sub + at, left, 0.0), axis=1, keepdims=True)
        scale = lax.rsqrt(pivots)
        scale = scale * (1.5 - 0.5 * pivots * scale * scale)
        panel = jnp.concatenate([left * scale, right * scale], axis=1)
        high, middle, low = thirds(panel)
        a = [x[:, :TB] for x in (high, high, middle, high, middle, low)]
        b = [high, middle, high, low, middle, high]
        a = jnp.concatenate(a, axis=0).astype(jnp.bfloat16)
        b = jnp.concatenate(b, axis=0).astype(jnp.bfloat16)
        update = dot(a, b, ((0,), (0,)))
        aug[...] = jnp.where(below >= at + PANEL, aug[...] - update, aug[...])
        aug[here, :] = panel

    lax.fori_loop(0, TB // PANEL, step, None)
    return aug[:, pl.ds(TB, TB)]


def factor_kernel(gram, out, aug):
    out[...] = factor(gram[...] * (1.0 / NODES), aug)


def inverse_factor(gram):
    vmem = pl.BlockSpec(memory_space=pltpu.MemorySpace.VMEM)
    return pl.pallas_call(
        factor_kernel,
        in_specs=[vmem],
        out_specs=vmem,
        out_shape=jax.ShapeDtypeStruct((TB, TB), jnp.float32),
        scratch_shapes=[pltpu.VMEM((TB, 2 * TB), jnp.float32)],
        compiler_params=PARAMS,
        name="factor",
    )(gram)


def encode_kernel(block, first, inverse, out, both):
    inv = tall(inverse[...])
    both[...] = fold(dot(inv, wide(first[...]), ((1,), (0,))))

    def step(h, _):
        for t in range(HEAD):
            where = tile_rows(h * HEAD + t)
            out[where, :] = times_transpose(block[where, :], inv)

    lax.fori_loop(0, ROWS // HEAD, step, None)


def rayleigh_kernel(projection, second, both, out):
    left = fold(dot(tall(second[...]), wide(projection[...] * (1.0 / NODES)), ((1,), (0,))))
    out[...] = times_transpose(left, tall(both[...]))


def relay(value, along):
    return lax.ppermute(value, AXES, pairs((0, 0, 0, along), (0, 0, 0, -along)))


def exchange(head, edge, carry):
    straight = relay(head, 1)
    first = {i: cross(edge, i, 0) for i in (2, 1, 3)}
    crossed = relay(head, -1)
    forwarded = relay(straight, 1)
    packed = pack(TB, [edge, first[1], first[3], first[2]], carry)
    second = {i: cross(packed, i, 1) for i in (2, 1, 3)}
    early = pack(HEAD * TB, [packed, second[2], second[3]])
    late = second[1]
    if carry:
        (late,) = call(sum_kernel, [packed, second[1], second[3], second[2]], [tiles_of(HEAD + 1)])
    theirs = [shift(early, dc=1), shift(late, dc=1)]
    return [straight, crossed, forwarded], [packed, late, second[3], second[2]] + theirs


def ring_sum(value, axis):
    two, one, three = (shift(value, **{"d" + axis: step}) for step in (2, 1, 3))
    return (value + two) + (one + three)


def steps(start_block, near_tiles, near_src, near_mask, far_tiles, far_src, far_mask, bound_count):
    *tiles, index = prepare(near_tiles, near_src, near_mask, far_tiles, far_src, far_mask)
    first = ((1.0 - CENTER) / HALF, -1.0 / HALF)
    later = (2.0 * first[0], 2.0 * first[1])

    *state, edge = start(bound_count, start_block)
    plan = (
        [("step", first, False), ("step", later, True), ("gram", later, True)]
        + [("step", first, False), ("step", later, True), ("step", later, True)]
        + [("last", (1.0, -1.0), False)]
    )
    carries = {3: "give", 4: "pass", 5: "take"}
    before = None
    for number, (kind, coefs, back) in enumerate(plan, 1):
        if kind == "last":
            block, edge = normalise(state, inverse, edge)
        halo, far = exchange(state[0], edge, number in (4, 7))
        base, v = apply_own(coefs, tiles, state, before if back else None, halo)
        if number == 6:
            inverse = inverse_factor(gram)
        if kind == "last":
            value = apply_last(coefs[1], index, tiles, base, v, halo[2], far, block)
        else:
            parts = [state[0], *halo[:2]]
            before = state
            state, edge, total = apply_rest(
                coefs[1], carries.get(number), index, bound_count, tiles, base, v, halo[2], far, parts
            )
            if total:
                (gram,) = total
    value = ring_sum(value, "z")
    second = inverse_factor(value[TB:])
    encodings, both = call(encode_kernel, [block, inverse, second], [BLOCK, SMALL])
    projection = value[:TB]
    projection = projection + shift(projection, dc=1)
    projection = ring_sum(ring_sum(projection, "x"), "y")
    (rayleigh,) = call(rayleigh_kernel, [projection, second, both], [SMALL])
    return encodings, rayleigh


def solution(mesh):
    rows = P(AXES)
    return jax.shard_map(
        steps,
        mesh=mesh,
        in_specs=(rows,) * 8,
        out_specs=(rows, P()),
        check_vma=False,
    )
```
